256 devices in a mesh: dp: 8 (over x, core), vocab: 16 (over z_hi, y), width: 2 (over z_lo).
Axes of the slice: x: 4, y: 4, z: 8 (z_hi: 4, z_lo: 2; z = z_hi * 2 + z_lo), core: 2. Of those that a mesh axis runs over, the one named last changes fastest.
Arguments:
- hidden: bfloat16 [8192, 5376], P(('dp', 'vocab'), 'width'), may hold values from -1000 to 1000, as said below
- rest_lse: bfloat16 [8192], P(('dp', 'vocab')), may hold values from 0 to 800
- token_ids: int32 [8192], P(('dp', 'vocab')), may hold values from 0 to 32767
- slab_offset: int32 [1], replicated, may hold values from 0 to 16384
- embedding: bfloat16 [16384, 5376], P('vocab', 'width'), may hold values from -0.078125 to 0.078125
- row_state: float32 [16384], P(('vocab', 'dp')), may hold values from 0.001 to 5, as said below
- col_state: float32 [5376], P('width'), may hold values from 0.003 to 0.3
Outputs:
- update: float32 [16384, 5376], P(('vocab', 'dp'), 'width')
- new_rows: float32 [16384], P(('vocab', 'dp'))
- new_cols: float32 [5376], P('width')
- row_mean: float32 [1], replicated
The draws below stay inside these ranges and needn't reach their ends.
Inputs may be any that keep to these rules, and one draw needn't show every extreme that they name: `hidden`: entries stay within the stated range. `row_state`: entries are positive.
All inputs are finite; a program needn't handle non-finite values.
Results may differ from the reference program's by a relative error of at most 0.0012.
Values may be sent and summed in bfloat16 or wider, within the bound.
A program may use at most 64 MiB of HBM per device.

```python
import math
import jax
import jax.numpy as jnp
from jax import lax

D = 5376
VOC_DEV = 1024
TOK_REP = 1024
SLAB = 16384
TOKENS = 8192
N_DP = 8


def draw_hidden(key, part):
    base = jax.random.normal(jax.random.fold_in(key, 10), (TOKENS, D), jnp.float32)
    base = jnp.clip(base, -6.0, 6.0)
    return base.astype(jnp.bfloat16)


def draw_rest_lse(key, part):
    factor = jnp.ones((TOKENS,), jnp.float32)
    log_rows = jnp.log(jnp.float32(SLAB))
    top_scale = jnp.sqrt(2.0 * log_rows)
    center = jnp.where(factor < top_scale, log_rows + 0.5 * factor, top_scale * factor)
    noise = jax.random.uniform(jax.random.fold_in(key, 31), (TOKENS,), jnp.float32, -2.5, 2.5)
    return (center + noise).astype(jnp.bfloat16)


def draw_row_state(key, part):
    noise_key = jax.random.fold_in(key, 21)
    position = (jnp.arange(SLAB, dtype=jnp.int32) % VOC_DEV).astype(jnp.float32) / VOC_DEV
    ramp = 0.05 * jnp.exp(jnp.log(10.0) * position)
    factor = jnp.exp(jax.random.uniform(noise_key, (SLAB,), jnp.float32, -1.2, 1.2))
    return (ramp * factor).astype(jnp.float32)


def set_ends(array, own_key, smallest, largest):
    longest = array.shape.index(max(array.shape))
    spots = []
    for shift in (0, 1):
        where = [jax.random.randint(jax.random.fold_in(own_key, axis), (), 0, length) for axis, length in enumerate(array.shape)]
        where[longest] = (where[longest] + shift) % array.shape[longest]
        spots.append(tuple(where))
    return array.at[spots[0]].set(smallest).at[spots[1]].set(largest)


def steps_of(stream_key, dims, shards, low, top_value):
    def one(dim, shards_of):
        heights = jax.random.uniform(jax.random.fold_in(jax.random.fold_in(stream_key, 6), dim), (shards_of,), jnp.float32, low / len(shards), top_value / len(shards))
        return jnp.repeat(jnp.exp(heights), dims[dim] // shards_of).reshape((-1,) + (1,) * (len(dims) - dim - 1))

    gain = one(*shards[0])
    for cut in shards[1:]:
        gain = gain * one(*cut)
    return gain


def gaussian(stream_key, dims, scale, limit, shards=(), held_as=jnp.bfloat16):
    entries = scale * jax.random.normal(stream_key, dims, jnp.float32)
    if shards:
        entries = entries * steps_of(stream_key, dims, shards, -0.22, 0.18)
    return jnp.clip(entries, -limit, limit).astype(held_as)


def setup_inputs(seed: int = 0) -> dict:
    arg_keys = jax.random.split(jax.random.key(seed), 8)
    return {
        "hidden": draw_hidden(jax.random.fold_in(arg_keys[7], 71), 0),
        "rest_lse": draw_rest_lse(jax.random.fold_in(arg_keys[7], 71), 0),
        "token_ids": set_ends(jax.random.randint(arg_keys[2], (TOKENS,), 0, 2 * SLAB), jax.random.fold_in(arg_keys[2], 1), 0, (2 * SLAB) - 1).astype(jnp.int32),
        "slab_offset": jax.random.randint(arg_keys[3], (1,), 0, SLAB + 1).astype(jnp.int32),
        "embedding": gaussian(arg_keys[4], (SLAB, D), D ** -0.5, 0.078125, ((0, 16), (1, 2))),
        "row_state": draw_row_state(jax.random.fold_in(arg_keys[7], 71), 0),
        "col_state": jnp.clip(jnp.exp(math.log(0.3) - 4.6051702 * jax.random.uniform(arg_keys[6], (D,), jnp.float32) ** steps_of(arg_keys[6], (D,), ((0, 2),), -0.2, 0.2)), 0.003, 0.3),
    }


def reference(hidden, rest_lse, token_ids, slab_offset, embedding, row_state, col_state):
    grad = jnp.zeros((SLAB, D), jnp.float32)
    row_index = jnp.arange(SLAB, dtype=jnp.int32)
    for replica in range(N_DP):
        lower = replica * TOK_REP
        states = hidden[lower:lower + TOK_REP]
        rest = rest_lse[lower:lower + TOK_REP].astype(jnp.float32)
        labels = token_ids[lower:lower + TOK_REP]
        logits = lax.dot_general(states, embedding, (((1,), (1,)), ((), ())), preferred_element_type=jnp.float32)
        top = lax.optimization_barrier(jnp.max(logits, axis=1))
        total = lax.optimization_barrier(jnp.sum(jnp.exp(logits - top[:, None]), axis=1))
        big = jnp.maximum(top, rest)
        lse = big + jnp.log(total * jnp.exp(top - big) + jnp.exp(rest - big))
        hit = labels[:, None] - slab_offset[0] == row_index[None, :]
        dlogits = (jnp.exp(logits - lse[:, None]) - hit.astype(jnp.float32)).astype(jnp.bfloat16)
        grad = grad + lax.dot_general(dlogits, states, (((0,), (0,)), ((), ())), preferred_element_type=jnp.float32)
    square = grad * grad + 1e-06
    row_sq = lax.optimization_barrier(jnp.sum(square, axis=1))
    col_sq = lax.optimization_barrier(jnp.sum(square, axis=0))
    new_rows = 0.9 * row_state + 0.1 * row_sq / D
    new_cols = 0.9 * col_state + 0.1 * col_sq / SLAB
    mean_rows = jnp.mean(new_rows)
    raw = grad * lax.rsqrt(new_rows[:, None] * new_cols[None, :] / mean_rows)
    rms = jnp.sqrt(jnp.mean(raw * raw))
    update = raw / jnp.maximum(1.0, rms / 0.1)
    return (update, new_rows, new_cols, jnp.reshape(mean_rows, (1,)))
```

```python
import functools

import jax
import jax.numpy as jnp
from jax import lax
from jax.experimental import pallas as pl
from jax.experimental.pallas import tpu as pltpu
from jax.sharding import Mesh
from jax.sharding import PartitionSpec as P

VOCAB = ("vocab_0", "vocab_1")
DP_VOCAB = ("dp_0", "dp_1", "vocab_0", "vocab_1")
VOCAB_DP = ("vocab_0", "vocab_1", "dp_0", "dp_1")
MESH = pl.DeviceIdType.MESH
F32 = jnp.float32
BF16 = jnp.bfloat16

SHARD = 64
CHUNK = 256
HALF = 128
ROWS = 1024
BLK = 128
K = 2688
TILES = K // 128
SLAB = 16384
FULL = 5376
TOKENS_TOTAL_TILES = 43
PER = 6
NW = 896
NP = K // NW


def kernel(hid, aux, emb, row_state, col_state,
           upd, nrows_out, ncols_out, mean_out,
           h0, h1, ev, ar, lown, lsend, lrecv, st, sr, lse,
           da, db, rpair, rsib, rdiag, part, ra, rb, fa, fb,
           rowp, rowx, vec, vr, ss, s2r, wv, qv, qx,
           local_sem, aux_s, aux_r, z_s, z_r, y_s, y_r, sib_s, sib_r, l_s, l_r,
           st_s, st_r, d_s, d_r, rs_s, rs_r, row_sem, v_s, v_r, s2_s, s2_r, w_s, w_r, q_sem):
    x = lax.axis_index("dp_0")
    c = lax.axis_index("dp_1")
    zh = lax.axis_index("vocab_0")
    y = lax.axis_index("vocab_1")
    w = lax.axis_index("width")
    d = x * 2 + c
    v = zh * 4 + y

    def plus(a, b):
        return lax.rem(a + b, 4)

    voc = [(oz, oy) for oz in range(4) for oy in range(4) if (oz, oy) != (0, 0)]
    dps = [(ox, oc) for ox in range(4) for oc in range(2) if (ox, oc) != (0, 0)]

    def to_voc(oz, oy):
        return {"vocab_0": plus(zh, oz), "vocab_1": plus(y, oy)}

    def to_dp(ox, oc):
        return {"dp_0": plus(x, ox), "dp_1": lax.rem(c + oc, 2)}

    pair = {"width": 1 - w}
    sib = {"dp_1": 1 - c}
    diag = {"width": 1 - w, "dp_1": 1 - c}
    zp, zm = {"vocab_0": plus(zh, 1)}, {"vocab_0": plus(zh, 3)}
    yp, ym = {"vocab_1": plus(y, 1)}, {"vocab_1": plus(y, 3)}
    xp, xm = {"dp_0": plus(x, 1)}, {"dp_0": plus(x, 3)}

    barrier = pltpu.get_barrier_semaphore()
    everyone = [to_voc(*o) for o in voc] + [to_dp(*o) for o in dps] + [pair, diag]
    for peer in everyone:
        pl.semaphore_signal(barrier, inc=1, device_id=peer, device_id_type=MESH)

    def slot_row(z, yy):
        return (z * 4 + lax.rem(yy + 2 * w, 4)) * SHARD

    def rows_of(z, yy, start=0, size=SHARD):
        at = pl.multiple_of(slot_row(z, yy) + start, 32)
        return h0.at[pl.ds(at, size)]

    load_emb = pltpu.make_async_copy(emb, ev, local_sem.at[0])
    load_emb.start()
    load_own = pltpu.make_async_copy(hid, rows_of(zh, y), local_sem.at[1])
    load_own.start()
    load_aux = pltpu.make_async_copy(aux, ar.at[zh * 4 + lax.rem(y + 2 * w, 4)], local_sem.at[2])
    load_aux.start()
    pl.semaphore_wait(barrier, len(everyone))

    sent = []

    def send(src, dst, s_sem, r_sem, peer, shared=False):
        copy = pltpu.make_async_remote_copy(
            src_ref=src, dst_ref=dst, send_sem=s_sem, recv_sem=r_sem,
            device_id=peer, device_id_type=MESH,
        )
        copy.start()
        if not shared:
            sent.append(copy)
        return copy

    zs = [zh, plus(zh, 3), plus(zh, 1), plus(zh, 2)]
    y1, y2 = [None] * 4, [None] * 4

    def y_first(j):
        z = zs[j]
        src = hid if j == 0 else rows_of(z, y)
        y1[j] = (
            send(src, rows_of(z, y), y_s.at[j, 0], y_r.at[j, 0], yp),
            send(src, rows_of(z, y), y_s.at[j, 1], y_r.at[j, 1], ym),
        )

    def y_second(j):
        z = zs[j]
        below, above = plus(y, 3), plus(y, 1)
        y1[j][0].wait_recv()
        one = rows_of(z, below, 0, 32)
        a = send(one, one, y_s.at[j, 2], y_r.at[j, 2], yp)
        y1[j][1].wait_recv()
        two = rows_of(z, above, 32, 32)
        b = send(two, two, y_s.at[j, 3], y_r.at[j, 3], ym)
        y2[j] = (a, b)

    sib_copies = [None] * 4

    def y_done(j):
        y2[j][0].wait_recv()
        y2[j][1].wait_recv()
        at = pl.ds(pl.multiple_of(zs[j] * CHUNK, CHUNK), CHUNK)
        sib_copies[j] = send(h0.at[at], h1.at[at], sib_s.at[j], sib_r.at[j], sib)

    own = rows_of(zh, y)
    z1p = send(hid, own, z_s.at[0], z_r.at[0], zp)
    z1m = send(hid, own, z_s.at[1], z_r.at[1], zm)
    y_first(0)
    load_aux.wait()
    mine = ar.at[zh * 4 + lax.rem(y + 2 * w, 4)]
    for oz, oy in voc:
        send(mine, mine, aux_s, aux_r, to_voc(oz, oy), True)
    load_own.wait()

    logit_copies = [None] * 4

    def logits_of(j):
        at = pl.ds(pl.multiple_of(zs[j] * CHUNK, CHUNK), CHUNK)

        @pl.loop(0, 2)
        def _(m):
            rows = pl.ds(pl.multiple_of(m * 512, 512), 512)
            both = lax.dot_general(
                ev[rows, :], h0[at, :], (((1,), (1,)), ((), ())), preferred_element_type=F32
            )
            lown[j, rows, :] = both[:, :HALF]
            lsend[j, rows, :] = both[:, HALF:]

        logit_copies[j] = send(lsend.at[j], lrecv.at[j], l_s.at[j], l_r.at[j], pair)

    def stats_of(j):
        logit_copies[j].wait_recv()

        def first(m, top):
            rows = pl.ds(pl.multiple_of(m * 256, 256), 256)
            both = lown[j, rows, :] + lrecv[j, rows, :]
            lown[j, rows, :] = both
            return jnp.maximum(top, jnp.max(both.reshape(32, 8, HALF), axis=0))

        top = lax.fori_loop(0, 4, first, jnp.full((8, HALF), -jnp.inf, F32))
        top = jnp.max(top, axis=0, keepdims=True)

        def second(m, total):
            rows = pl.ds(pl.multiple_of(m * 256, 256), 256)
            part_sum = jnp.exp(lown[j, rows, :] - top)
            return total + jnp.sum(part_sum.reshape(32, 8, HALF), axis=0)

        total = lax.fori_loop(0, 4, second, jnp.zeros((8, HALF), F32))
        st[zs[j]] = top
        st[zs[j] + 4] = jnp.sum(total, axis=0, keepdims=True)

    y_second(0)
    z1p.wait_recv()
    low = rows_of(plus(zh, 3), y, 0, 32)
    z2p = send(low, low, z_s.at[2], z_r.at[2], zp)
    y_first(1)
    z1m.wait_recv()
    high = rows_of(plus(zh, 1), y, 32, 32)
    z2m = send(high, high, z_s.at[3], z_r.at[3], zm)
    y_first(2)
    y_done(0)
    load_emb.wait()
    logits_of(0)
    z2p.wait_recv()
    z2m.wait_recv()
    y_first(3)
    y_second(1)
    y_second(2)
    y_done(1)
    logits_of(1)
    y_second(3)
    stats_of(0)
    y_done(2)
    logits_of(2)
    stats_of(1)
    y_done(3)
    logits_of(3)
    stats_of(2)
    stats_of(3)

    for k, (oz, oy) in enumerate(voc):
        send(st, sr.at[k], st_s, st_r, to_voc(oz, oy), True)
    pltpu.make_async_copy(ar.at[pl.ds(0, 15)], ar.at[pl.ds(0, 15)], aux_r).wait()
    pltpu.make_async_copy(sr, sr, st_r).wait()
    for zz in range(4):
        top = st[zz]
        for k in range(15):
            top = jnp.maximum(top, sr[k, zz])
        total = st[zz + 4] * jnp.exp(st[zz] - top)
        for k in range(15):
            total = total + sr[k, zz + 4] * jnp.exp(sr[k, zz] - top)
        rest = ar[zz * 4, 0:1, :] + ar[zz * 4 + 1, 0:1, :]
        big = jnp.maximum(top, rest)
        lse[zz] = big + jnp.log(total * jnp.exp(top - big) + jnp.exp(rest - big))

    d_copies = [None] * 4
    for j in range(4):
        z = zs[j]
        shift = lse[z]
        label = ar[z * 4, 1:2, :] + ar[z * 4 + 1, 1:2, :] - (v * ROWS).astype(F32)
        lane_row = lax.broadcasted_iota(jnp.int32, (BLK, HALF), 0).astype(F32)

        @pl.loop(0, 4)
        def _(xr):
            base = plus(x, xr) * 2 * BLK
            for core, dst in ((c, da), (1 - c, db)):
                row0 = pl.multiple_of(base + core * BLK, BLK)
                hit = (lane_row == label - row0.astype(F32)).astype(F32)
                dst[j, xr] = (jnp.exp(lown[j, pl.ds(row0, BLK), :] - shift) - hit).astype(BF16)

        d_copies[j] = (
            send(da.at[j], rpair.at[j], d_s.at[j, 0], d_r.at[j, 0], pair),
            send(db.at[j], rdiag.at[j], d_s.at[j, 1], d_r.at[j, 1], diag),
            send(db.at[j], rsib.at[j], d_s.at[j, 2], d_r.at[j, 2], sib),
        )

    def grad_piece(j, cols):
        at = pl.ds(pl.multiple_of(zs[j] * CHUNK, CHUNK), CHUNK)
        left = jnp.concatenate([da[j].reshape(512, HALF), rpair[j].reshape(512, HALF)], axis=1)
        right = jnp.concatenate([rsib[j].reshape(512, HALF), rdiag[j].reshape(512, HALF)], axis=1)
        both = jnp.dot(left, h0[at, cols], preferred_element_type=F32)
        both = both + jnp.dot(right, h1[at, cols], preferred_element_type=F32)
        both = both.reshape(4, BLK, NW)
        if j == 0:
            part[:, :, cols] = both
        else:
            part[:, :, cols] = part[:, :, cols] + both

    for j in range(3):
        for copy in d_copies[j]:
            copy.wait_recv()
        sib_copies[j].wait_recv()

        @pl.loop(0, NP)
        def _(n):
            grad_piece(j, pl.ds(pl.multiple_of(n * NW, 128), NW))

    for copy in d_copies[3]:
        copy.wait_recv()
    sib_copies[3].wait_recv()

    relay, whole = [None] * NP, [None] * NP

    def send_whole(n):
        cols = pl.ds(n * NW, NW)
        relay[n][0].wait_recv()
        part[1, 0:64, cols] = part[1, 0:64, cols] + ra[:, cols]
        one = send(part.at[1, :, cols], fa.at[:, cols], rs_s.at[n, 2], rs_r.at[n, 2], xp)
        relay[n][1].wait_recv()
        part[3, 64:128, cols] = part[3, 64:128, cols] + rb[:, cols]
        two = send(part.at[3, :, cols], fb.at[:, cols], rs_s.at[n, 3], rs_r.at[n, 3], xm)
        whole[n] = (one, two)

    for n in range(NP):
        cols = pl.ds(n * NW, NW)
        grad_piece(3, cols)
        relay[n] = (
            send(part.at[2, pl.ds(0, 64), cols], ra.at[:, cols], rs_s.at[n, 0], rs_r.at[n, 0], xp),
            send(part.at[2, pl.ds(64, 64), cols], rb.at[:, cols], rs_s.at[n, 1], rs_r.at[n, 1], xm),
        )
        if n > 0:
            send_whole(n - 1)
    send_whole(NP - 1)

    row_sum = jnp.zeros((BLK, 128), F32)
    vec[...] = jnp.zeros_like(vec)

    def slot(i):
        return i // PER, pl.ds(i % PER, 1)

    for t in range(TILES):
        if (t * 128) % NW == 0:
            for copy in whole[t * 128 // NW]:
                copy.wait_recv()
        cols = pl.ds(t * 128, 128)
        g = part[0, :, cols] + fa[:, cols] + fb[:, cols]
        part[0, :, cols] = g
        square = g * g + 1e-06
        row_sum = row_sum + square
        p, r = slot(t)
        vec[p, r, :] = jnp.sum(square, axis=0, keepdims=True)
    rowp[...] = row_sum
    row_copy = send(rowp, rowx, row_sem.at[0], row_sem.at[1], pair)
    state = jnp.transpose(jnp.broadcast_to(row_state[...], (BLK, 128)))
    row_copy.wait_recv()
    row_sq = jnp.sum(rowp[...] + rowx[...], axis=1, keepdims=True)
    new_rows = 0.9 * state + 0.1 * jnp.broadcast_to(row_sq, (BLK, 128)) / FULL
    nrows_out[...] = jnp.transpose(new_rows)[0:1, :]
    inverse = 1.0 / new_rows
    for t in range(TILES):
        g = part[0, :, pl.ds(t * 128, 128)]
        p, r = slot(TILES + t)
        vec[p, r, :] = jnp.sum(g * g * inverse, axis=0, keepdims=True)
    p, r = slot(2 * TILES)
    vec[p, r, :] = jnp.sum(new_rows, axis=0, keepdims=True)

    for k, (ox, oc) in enumerate(dps):
        piece = plus(x, ox) * 2 + lax.rem(c + oc, 2)
        send(vec.at[piece], vr.at[k], v_s, v_r, to_dp(ox, oc), True)
    pltpu.make_async_copy(vr, vr, v_r).wait()
    total = vec[d]
    for k in range(7):
        total = total + vr[k]
    ss[...] = total
    s2r[v] = total
    for oz, oy in voc:
        send(ss, s2r.at[v], s2_s, s2_r, to_voc(oz, oy), True)
    pltpu.make_async_copy(s2r.at[pl.ds(0, 15)], s2r.at[pl.ds(0, 15)], s2_r).wait()
    total = s2r[0]
    for k in range(1, 16):
        total = total + s2r[k]
    wv[d] = total
    for ox, oc in dps:
        send(wv.at[d], wv.at[d], w_s, w_r, to_dp(ox, oc), True)
    pltpu.make_async_copy(wv.at[pl.ds(0, 7)], wv.at[pl.ds(0, 7)], w_r).wait()

    p, r = slot(2 * TILES)
    mean = wv[p, r, :] / SLAB
    mean_out[...] = mean
    weighted = jnp.zeros((1, 128), F32)
    for t in range(TILES):
        cols = pl.ds(t * 128, 128)
        p, r = slot(t)
        new_cols = 0.9 * col_state[:, cols] + 0.1 * wv[p, r, :] / SLAB
        ncols_out[:, cols] = new_cols
        p, r = slot(TILES + t)
        weighted = weighted + wv[p, r, :] / new_cols
    weighted = jnp.sum(weighted, axis=1, keepdims=True) * mean
    qv[...] = jnp.broadcast_to(weighted, (8, 128))
    q_copy = send(qv, qx, q_sem.at[0], q_sem.at[1], pair)
    row_factor = lax.rsqrt(new_rows)
    q_copy.wait_recv()
    rms = jnp.sqrt((qv[0:1, :] + qx[0:1, :]) / (SLAB * FULL))
    clip = 1.0 / jnp.maximum(1.0, rms / 0.1)
    for t in range(TILES):
        cols = pl.ds(t * 128, 128)
        col_factor = lax.rsqrt(ncols_out[:, cols] / mean) * clip
        upd[:, cols] = part[0, :, cols] * row_factor * col_factor

    for copy in sent:
        copy.wait_send()
    pltpu.make_async_copy(ar.at[pl.ds(0, 15)], ar.at[pl.ds(0, 15)], aux_s).wait()
    pltpu.make_async_copy(sr, sr, st_s).wait()
    pltpu.make_async_copy(vr, vr, v_s).wait()
    pltpu.make_async_copy(s2r.at[pl.ds(0, 15)], s2r.at[pl.ds(0, 15)], s2_s).wait()
    pltpu.make_async_copy(wv.at[pl.ds(0, 7)], wv.at[pl.ds(0, 7)], w_s).wait()


def per_device(hidden, rest_lse, token_ids, slab_offset, embedding, row_state, col_state):
    odd = lax.rem(lax.axis_index("vocab_1"), 2)
    lines = jnp.stack([rest_lse.astype(F32), (token_ids - slab_offset[0]).astype(F32)])
    left = jnp.where(odd == 0, lines, 0.0)
    right = jnp.where(odd == 0, 0.0, lines)
    aux = jnp.pad(jnp.concatenate([left, right], axis=1), ((0, 6), (0, 0)))
    any_spec = pl.BlockSpec(memory_space=pl.ANY)
    vmem = pl.BlockSpec(memory_space=pltpu.VMEM)
    dma = pltpu.SemaphoreType.DMA
    V = pltpu.VMEM
    scratch = [
        V((ROWS, K), BF16), V((ROWS, K), BF16), V((ROWS, K), BF16),
        V((16, 8, 128), F32),
        V((4, ROWS, HALF), F32), V((4, ROWS, HALF), F32), V((4, ROWS, HALF), F32),
        V((8, 1, 128), F32), V((15, 8, 1, 128), F32), V((4, 1, 128), F32),
        V((4, 4, BLK, HALF), BF16), V((4, 4, BLK, HALF), BF16),
        V((4, 4, BLK, HALF), BF16), V((4, 4, BLK, HALF), BF16), V((4, 4, BLK, HALF), BF16),
        V((4, BLK, K), F32),
        V((64, K), F32), V((64, K), F32), V((BLK, K), F32), V((BLK, K), F32),
        V((BLK, 128), F32), V((BLK, 128), F32),
        V((8, 8, 128), F32), V((7, 8, 128), F32), V((8, 128), F32),
        V((16, 8, 128), F32), V((8, 8, 128), F32), V((8, 128), F32), V((8, 128), F32),
        dma((3,)), dma, dma, dma((4,)), dma((4,)), dma((4, 4)), dma((4, 4)),
        dma((4,)), dma((4,)), dma((4,)), dma((4,)), dma, dma, dma((4, 3)), dma((4, 3)),
        dma((NP, 4)), dma((NP, 4)), dma((2,)), dma, dma, dma, dma, dma, dma, dma((2,)),
    ]
    update, new_rows, new_cols, mean = pl.pallas_call(
        kernel,
        out_shape=(
            jax.ShapeDtypeStruct((BLK, K), F32),
            jax.ShapeDtypeStruct((1, BLK), F32),
            jax.ShapeDtypeStruct((1, K), F32),
            jax.ShapeDtypeStruct((1, 128), F32),
        ),
        in_specs=[any_spec, any_spec, any_spec, vmem, vmem],
        out_specs=(vmem, vmem, vmem, vmem),
        scratch_shapes=scratch,
        compiler_params=pltpu.CompilerParams(
            collective_id=0, has_side_effects=True, vmem_limit_bytes=62 * 1024 * 1024
        ),
    )(hidden, aux, embedding, row_state.reshape(1, BLK), col_state.reshape(1, K))
    return update, new_rows.reshape(BLK), new_cols.reshape(K), mean[0, :1]


def solution(mesh):
    finer = Mesh(
        mesh.devices.reshape(4, 2, 4, 4, mesh.shape["width"]),
        ("dp_0", "dp_1", "vocab_0", "vocab_1", "width"),
    )
    placed = (
        P(DP_VOCAB, "width"),
        P(DP_VOCAB),
        P(DP_VOCAB),
        P(),
        P(VOCAB, "width"),
        P(VOCAB_DP),
        P("width"),
    )
    return jax.shard_map(
        per_device,
        mesh=finer,
        in_specs=placed,
        out_specs=(P(VOCAB_DP, "width"), P(VOCAB_DP), P("width"), P()),
        check_vma=False,
    )
```

```python
import functools

import jax
import jax.numpy as jnp
from jax import lax
from jax.experimental import pallas as pl
from jax.experimental.pallas import tpu as pltpu
from jax.sharding import Mesh
from jax.sharding import PartitionSpec as P

VOCAB = ("vocab_0", "vocab_1")
DP_VOCAB = ("dp_0", "dp_1", "vocab_0", "vocab_1")
VOCAB_DP = ("vocab_0", "vocab_1", "dp_0", "dp_1")
MESH = pl.DeviceIdType.MESH
F32 = jnp.float32
BF16 = jnp.bfloat16

SHARD = 64
CHUNK = 256
HALF = 128
ROWS = 1024
BLK = 128
K = 2688
TILES = K // 128
SLAB = 16384
FULL = 5376
PER = 6
NW = 896
NP = K // NW


def kernel(hid, emb, rest, ids, offset, row_state, col_state,
           g_out, row_out, col_out, nrows_out, ncols_out, mean_out,
           h0, h1, ev, lown, lsend, lrecv, sr, lse,
           da, db, rpair, rsib, rdiag, part, ra, rb, fa, fb,
           rowp, rowx, vec, vr, ss, s2r, wv, qv, qx,
           local_sem, z_s, z_r, y_s, y_r, sib_s, sib_r, l_s, l_r,
           st_s, st_r, d_s, d_r, rs_s, rs_r, row_sem, v_s, v_r, s2_s, s2_r, w_s, w_r, q_sem):
    x = lax.axis_index("dp_0")
    c = lax.axis_index("dp_1")
    zh = lax.axis_index("vocab_0")
    y = lax.axis_index("vocab_1")
    w = lax.axis_index("width")
    d = x * 2 + c
    v = zh * 4 + y

    def plus(a, b):
        return lax.rem(a + b, 4)

    voc = [(oz, oy) for oz in range(4) for oy in range(4) if (oz, oy) != (0, 0)]
    dps = [(ox, oc) for ox in range(4) for oc in range(2) if (ox, oc) != (0, 0)]

    def to_voc(oz, oy):
        return {"vocab_0": plus(zh, oz), "vocab_1": plus(y, oy)}

    def to_dp(ox, oc):
        return {"dp_0": plus(x, ox), "dp_1": lax.rem(c + oc, 2)}

    pair = {"width": 1 - w}
    sib = {"dp_1": 1 - c}
    diag = {"width": 1 - w, "dp_1": 1 - c}
    zp, zm = {"vocab_0": plus(zh, 1)}, {"vocab_0": plus(zh, 3)}
    yp, ym = {"vocab_1": plus(y, 1)}, {"vocab_1": plus(y, 3)}
    xp, xm = {"dp_0": plus(x, 1)}, {"dp_0": plus(x, 3)}

    barrier = pltpu.get_barrier_semaphore()
    everyone = [zp, zm, yp, ym, xp, xm, sib, pair]
    for peer in everyone:
        pl.semaphore_signal(barrier, inc=1, device_id=peer, device_id_type=MESH)

    def slot_row(z, yy):
        return (z * 4 + lax.rem(yy + 2 * w, 4)) * SHARD

    def rows_of(z, yy, start=0, size=SHARD):
        at = pl.multiple_of(slot_row(z, yy) + start, 32)
        return h0.at[pl.ds(at, size)]

    load_emb = pltpu.make_async_copy(emb, ev, local_sem.at[0])
    load_emb.start()
    load_own = pltpu.make_async_copy(hid, rows_of(zh, y), local_sem.at[1])
    load_own.start()
    lane_odd = lax.broadcasted_iota(jnp.int32, (1, 128), 1) // 64
    side = lane_odd == lax.rem(y, 2)
    line = rest[...].astype(F32)
    sr[0, 8] = jnp.where(side, jnp.concatenate([line, line], axis=1), 0.0)
    line = (ids[...] - offset[0]).astype(F32)
    sr[0, 9] = jnp.where(side, jnp.concatenate([line, line], axis=1), 0.0)
    pl.semaphore_wait(barrier, len(everyone))

    sent = []

    def send(src, dst, s_sem, r_sem, peer, shared=False):
        copy = pltpu.make_async_remote_copy(
            src_ref=src, dst_ref=dst, send_sem=s_sem, recv_sem=r_sem,
            device_id=peer, device_id_type=MESH,
        )
        copy.start()
        if not shared:
            sent.append(copy)
        return copy

    zs = [zh, plus(zh, 3), plus(zh, 1), plus(zh, 2)]
    y1, y2 = [None] * 4, [None] * 4

    def y_first(j):
        z = zs[j]
        src = hid if j == 0 else rows_of(z, y)
        y1[j] = (
            send(src, rows_of(z, y), y_s.at[j, 0], y_r.at[j, 0], yp),
            send(src, rows_of(z, y), y_s.at[j, 1], y_r.at[j, 1], ym),
        )

    def y_second(j):
        z = zs[j]
        below, above = plus(y, 3), plus(y, 1)
        y1[j][0].wait_recv()
        one = rows_of(z, below, 0, 32)
        a = send(one, one, y_s.at[j, 2], y_r.at[j, 2], yp)
        y1[j][1].wait_recv()
        two = rows_of(z, above, 32, 32)
        b = send(two, two, y_s.at[j, 3], y_r.at[j, 3], ym)
        y2[j] = (a, b)

    sib_copies = [None] * 4

    def y_done(j):
        y2[j][0].wait_recv()
        y2[j][1].wait_recv()
        at = pl.ds(pl.multiple_of(zs[j] * CHUNK, CHUNK), CHUNK)
        sib_copies[j] = send(h0.at[at], h1.at[at], sib_s.at[j], sib_r.at[j], sib)

    own = rows_of(zh, y)
    z1p = send(hid, own, z_s.at[0], z_r.at[0], zp)
    z1m = send(hid, own, z_s.at[1], z_r.at[1], zm)
    y_first(0)
    load_own.wait()

    logit_copies = [None] * 4

    def logits_of(j):
        at = pl.ds(pl.multiple_of(zs[j] * CHUNK, CHUNK), CHUNK)

        @pl.loop(0, 2)
        def _(m):
            rows = pl.ds(pl.multiple_of(m * 512, 512), 512)
            both = lax.dot_general(
                ev[rows, :], h0[at, :], (((1,), (1,)), ((), ())), preferred_element_type=F32
            )
            lown[j, rows, :] = both[:, :HALF]
            lsend[j, rows, :] = both[:, HALF:]

        logit_copies[j] = send(lsend.at[j], lrecv.at[j], l_s.at[j], l_r.at[j], pair)

    def stats_of(j):
        logit_copies[j].wait_recv()

        def first(m, top):
            rows = pl.ds(pl.multiple_of(m * 256, 256), 256)
            both = lown[j, rows, :] + lrecv[j, rows, :]
            lown[j, rows, :] = both
            return jnp.maximum(top, jnp.max(both.reshape(32, 8, HALF), axis=0))

        top = lax.fori_loop(0, 4, first, jnp.full((8, HALF), -jnp.inf, F32))
        top = jnp.max(top, axis=0, keepdims=True)

        def second(m, total):
            rows = pl.ds(pl.multiple_of(m * 256, 256), 256)
            part_sum = jnp.exp(lown[j, rows, :] - top)
            return total + jnp.sum(part_sum.reshape(32, 8, HALF), axis=0)

        total = lax.fori_loop(0, 4, second, jnp.zeros((8, HALF), F32))
        sr[0, zs[j]] = top
        sr[0, zs[j] + 4] = jnp.sum(total, axis=0, keepdims=True)

    y_second(0)
    z1p.wait_recv()
    low = rows_of(plus(zh, 3), y, 0, 32)
    z2p = send(low, low, z_s.at[2], z_r.at[2], zp)
    y_first(1)
    z1m.wait_recv()
    high = rows_of(plus(zh, 1), y, 32, 32)
    z2m = send(high, high, z_s.at[3], z_r.at[3], zm)
    y_first(2)
    y_done(0)
    load_emb.wait()
    logits_of(0)
    y_second(1)
    z2p.wait_recv()
    z2m.wait_recv()
    y_second(2)
    y_first(3)
    y_done(1)
    logits_of(1)
    stats_of(0)
    y_done(2)
    logits_of(2)
    y_second(3)
    stats_of(1)
    y_done(3)
    logits_of(3)
    stats_of(2)
    stats_of(3)

    for oz, oy in voc:
        send(sr.at[0], sr.at[oz * 4 + oy], st_s, st_r, to_voc(oz, oy), True)
    pltpu.make_async_copy(sr.at[pl.ds(1, 15)], sr.at[pl.ds(1, 15)], st_r).wait()

    def given(z, row):
        from_z = lax.rem(zh + 4 - z, 4) * 4
        one = from_z + lax.rem(y + 4 - 2 * w, 4)
        two = from_z + lax.rem(y + 3 - 2 * w, 4)
        return sr[one, row] + sr[two, row]

    for zz in range(4):
        top = sr[0, zz]
        for k in range(1, 16):
            top = jnp.maximum(top, sr[k, zz])
        total = sr[0, zz + 4] * jnp.exp(sr[0, zz] - top)
        for k in range(1, 16):
            total = total + sr[k, zz + 4] * jnp.exp(sr[k, zz] - top)
        other = given(zz, 8)
        big = jnp.maximum(top, other)
        lse[zz] = big + jnp.log(total * jnp.exp(top - big) + jnp.exp(other - big))

    d_copies = [None] * 4
    for j in range(4):
        z = zs[j]
        shift = lse[z]
        label = given(z, 9) - (v * ROWS).astype(F32)
        lane_row = lax.broadcasted_iota(jnp.int32, (BLK, HALF), 0).astype(F32)

        @pl.loop(0, 4)
        def _(xr):
            base = plus(x, xr) * 2 * BLK
            for core, dst in ((c, da), (1 - c, db)):
                row0 = pl.multiple_of(base + core * BLK, BLK)
                hit = (lane_row == label - row0.astype(F32)).astype(F32)
                dst[j, xr] = (jnp.exp(lown[j, pl.ds(row0, BLK), :] - shift) - hit).astype(BF16)

        d_copies[j] = (
            send(da.at[j], rpair.at[j], d_s.at[j, 0], d_r.at[j, 0], pair),
            send(db.at[j], rdiag.at[j], d_s.at[j, 1], d_r.at[j, 1], diag),
            send(db.at[j], rsib.at[j], d_s.at[j, 2], d_r.at[j, 2], sib),
        )

    def grad_piece(j, cols):
        at = pl.ds(pl.multiple_of(zs[j] * CHUNK, CHUNK), CHUNK)
        left = jnp.concatenate([da[j].reshape(512, HALF), rpair[j].reshape(512, HALF)], axis=1)
        right = jnp.concatenate([rsib[j].reshape(512, HALF), rdiag[j].reshape(512, HALF)], axis=1)
        both = jnp.dot(left, h0[at, cols], preferred_element_type=F32)
        both = both + jnp.dot(right, h1[at, cols], preferred_element_type=F32)
        both = both.reshape(4, BLK, NW)
        if j == 0:
            part[:, :, cols] = both
        else:
            part[:, :, cols] = part[:, :, cols] + both

    for j in range(3):
        for copy in d_copies[j]:
            copy.wait_recv()
        sib_copies[j].wait_recv()

        @pl.loop(0, NP)
        def _(n):
            grad_piece(j, pl.ds(pl.multiple_of(n * NW, 128), NW))

    for copy in d_copies[3]:
        copy.wait_recv()
    sib_copies[3].wait_recv()

    relay, whole = [None] * NP, [None] * NP

    def send_whole(n):
        cols = pl.ds(n * NW, NW)
        relay[n][0].wait_recv()
        part[1, 0:64, cols] = part[1, 0:64, cols] + ra[:, cols]
        one = send(part.at[1, :, cols], fa.at[:, cols], rs_s.at[n, 2], rs_r.at[n, 2], xp)
        relay[n][1].wait_recv()
        part[3, 64:128, cols] = part[3, 64:128, cols] + rb[:, cols]
        two = send(part.at[3, :, cols], fb.at[:, cols], rs_s.at[n, 3], rs_r.at[n, 3], xm)
        whole[n] = (one, two)

    for n in range(NP):
        cols = pl.ds(n * NW, NW)
        grad_piece(3, cols)
        relay[n] = (
            send(part.at[2, pl.ds(0, 64), cols], ra.at[:, cols], rs_s.at[n, 0], rs_r.at[n, 0], xp),
            send(part.at[2, pl.ds(64, 64), cols], rb.at[:, cols], rs_s.at[n, 1], rs_r.at[n, 1], xm),
        )
        if n > 0:
            send_whole(n - 1)
    send_whole(NP - 1)

    row_sum = jnp.zeros((BLK, 128), F32)
    vec[...] = jnp.zeros_like(vec)

    def slot(i):
        return i // PER, pl.ds(i % PER, 1)

    for t in range(TILES):
        if (t * 128) % NW == 0:
            for copy in whole[t * 128 // NW]:
                copy.wait_recv()
        cols = pl.ds(t * 128, 128)
        g = part[0, :, cols] + fa[:, cols] + fb[:, cols]
        g_out[:, cols] = g
        square = g * g + 1e-06
        row_sum = row_sum + square
        p, r = slot(t)
        vec[p, r, :] = jnp.sum(square, axis=0, keepdims=True)
    rowp[...] = row_sum
    row_copy = send(rowp, rowx, row_sem.at[0], row_sem.at[1], pair)
    state = jnp.transpose(jnp.broadcast_to(row_state[...], (BLK, 128)))
    row_copy.wait_recv()
    row_sq = jnp.sum(rowp[...] + rowx[...], axis=1, keepdims=True)
    new_rows = 0.9 * state + 0.1 * jnp.broadcast_to(row_sq, (BLK, 128)) / FULL
    nrows_out[...] = jnp.transpose(new_rows)[0:1, :]
    row_out[...] = jnp.transpose(lax.rsqrt(new_rows))[0:1, :]
    inverse = 1.0 / new_rows
    for t in range(TILES):
        g = g_out[:, pl.ds(t * 128, 128)]
        p, r = slot(TILES + t)
        vec[p, r, :] = jnp.sum(g * g * inverse, axis=0, keepdims=True)
    p, r = slot(2 * TILES)
    vec[p, r, :] = jnp.sum(new_rows, axis=0, keepdims=True)

    for k, (ox, oc) in enumerate(dps):
        piece = plus(x, ox) * 2 + lax.rem(c + oc, 2)
        send(vec.at[piece], vr.at[k], v_s, v_r, to_dp(ox, oc), True)
    pltpu.make_async_copy(vr, vr, v_r).wait()
    total = vec[d]
    for k in range(7):
        total = total + vr[k]
    ss[...] = total
    s2r[v] = total
    for oz, oy in voc:
        send(ss, s2r.at[v], s2_s, s2_r, to_voc(oz, oy), True)
    pltpu.make_async_copy(s2r.at[pl.ds(0, 15)], s2r.at[pl.ds(0, 15)], s2_r).wait()
    total = s2r[0]
    for k in range(1, 16):
        total = total + s2r[k]
    wv[d] = total
    for ox, oc in dps:
        send(wv.at[d], wv.at[d], w_s, w_r, to_dp(ox, oc), True)
    pltpu.make_async_copy(wv.at[pl.ds(0, 7)], wv.at[pl.ds(0, 7)], w_r).wait()

    p, r = slot(2 * TILES)
    mean = wv[p, r, :] / SLAB
    mean_out[...] = mean
    weighted = jnp.zeros((1, 128), F32)
    for t in range(TILES):
        p, r = slot(t)
        new_cols = 0.9 * col_state[t:t + 1, :] + 0.1 * wv[p, r, :] / SLAB
        ncols_out[t:t + 1, :] = new_cols
        p, r = slot(TILES + t)
        weighted = weighted + wv[p, r, :] / new_cols
    weighted = jnp.sum(weighted, axis=1, keepdims=True) * mean
    qv[...] = jnp.broadcast_to(weighted, (8, 128))
    q_copy = send(qv, qx, q_sem.at[0], q_sem.at[1], pair)
    q_copy.wait_recv()
    rms = jnp.sqrt((qv[0:1, :] + qx[0:1, :]) / (SLAB * FULL))
    clip = 1.0 / jnp.maximum(1.0, rms / 0.1)
    col_out[...] = lax.rsqrt(ncols_out[...] / mean) * clip

    for copy in sent:
        copy.wait_send()
    pltpu.make_async_copy(sr.at[pl.ds(1, 15)], sr.at[pl.ds(1, 15)], st_s).wait()
    pltpu.make_async_copy(vr, vr, v_s).wait()
    pltpu.make_async_copy(s2r.at[pl.ds(0, 15)], s2r.at[pl.ds(0, 15)], s2_s).wait()
    pltpu.make_async_copy(wv.at[pl.ds(0, 7)], wv.at[pl.ds(0, 7)], w_s).wait()


def per_device(hidden, rest_lse, token_ids, slab_offset, embedding, row_state, col_state):
    any_spec = pl.BlockSpec(memory_space=pl.ANY)
    vmem = pl.BlockSpec(memory_space=pltpu.VMEM)
    dma = pltpu.SemaphoreType.DMA
    V = pltpu.VMEM
    scratch = [
        V((ROWS, K), BF16), V((ROWS, K), BF16), V((ROWS, K), BF16),
        V((4, ROWS, HALF), F32), V((4, ROWS, HALF), F32), V((4, ROWS, HALF), F32),
        V((16, 10, 1, 128), F32), V((4, 1, 128), F32),
        V((4, 4, BLK, HALF), BF16), V((4, 4, BLK, HALF), BF16),
        V((4, 4, BLK, HALF), BF16), V((4, 4, BLK, HALF), BF16), V((4, 4, BLK, HALF), BF16),
        V((4, BLK, K), F32),
        V((64, K), F32), V((64, K), F32), V((BLK, K), F32), V((BLK, K), F32),
        V((BLK, 128), F32), V((BLK, 128), F32),
        V((8, 8, 128), F32), V((7, 8, 128), F32), V((8, 128), F32),
        V((16, 8, 128), F32), V((8, 8, 128), F32), V((8, 128), F32), V((8, 128), F32),
        dma((2,)), dma((4,)), dma((4,)), dma((4, 4)), dma((4, 4)),
        dma((4,)), dma((4,)), dma((4,)), dma((4,)), dma, dma, dma((4, 3)), dma((4, 3)),
        dma((NP, 4)), dma((NP, 4)), dma((2,)), dma, dma, dma, dma, dma, dma, dma((2,)),
    ]
    g, row_factor, col_factor, new_rows, new_cols, mean = pl.pallas_call(
        kernel,
        out_shape=(
            jax.ShapeDtypeStruct((BLK, K), F32),
            jax.ShapeDtypeStruct((1, BLK), F32),
            jax.ShapeDtypeStruct((TILES, 128), F32),
            jax.ShapeDtypeStruct((1, BLK), F32),
            jax.ShapeDtypeStruct((TILES, 128), F32),
            jax.ShapeDtypeStruct((1, 128), F32),
        ),
        in_specs=[any_spec, any_spec, vmem, vmem, pl.BlockSpec(memory_space=pltpu.SMEM), vmem, vmem],
        out_specs=(vmem,) * 6,
        scratch_shapes=scratch,
        compiler_params=pltpu.CompilerParams(
            collective_id=0, has_side_effects=True, vmem_limit_bytes=62 * 1024 * 1024
        ),
    )(
        hidden, embedding, rest_lse.reshape(1, SHARD), token_ids.reshape(1, SHARD), slab_offset,
        row_state.reshape(1, BLK), col_state.reshape(TILES, 128),
    )
    update = g * row_factor.reshape(BLK, 1) * col_factor.reshape(1, K)
    return update, new_rows.reshape(BLK), new_cols.reshape(K), mean[0, :1]


def solution(mesh):
    finer = Mesh(
        mesh.devices.reshape(4, 2, 4, 4, mesh.shape["width"]),
        ("dp_0", "dp_1", "vocab_0", "vocab_1", "width"),
    )
    placed = (
        P(DP_VOCAB, "width"),
        P(DP_VOCAB),
        P(DP_VOCAB),
        P(),
        P(VOCAB, "width"),
        P(VOCAB_DP),
        P("width"),
    )
    return jax.shard_map(
        per_device,
        mesh=finer,
        in_specs=placed,
        out_specs=(P(VOCAB_DP, "width"), P(VOCAB_DP), P("width"), P()),
        check_vma=False,
    )
```
